32 devices in a mesh: tensor: 4 (over z), dp: 4 (over y, x), replica: 2 (over core).
Axes of the slice: x: 2, y: 2, z: 4, core: 2. Of those that a mesh axis runs over, the one named last changes fastest.
Arguments:
- states: bfloat16 [8, 256, 4096], P(('dp', 'replica')), may hold values from -6 to 6
- norm_gain: float32 [4096], replicated, may hold values from 0.26 to 4.4
- gate_up: bfloat16 [4096, 2, 14336], P('replica', None, 'tensor'), may hold values from -0.09375 to 0.09375
- cotangent: bfloat16 [8, 256, 14336], P(('dp', 'replica'), None, 'tensor'), may hold values from -120 to 120
- prompt: bfloat16 [32, 4096], replicated, may hold values from -6 to 6
- step_sizes: float32 [3], replicated, may hold values from 0.3 to 1
- insert_at: int32 [8], P(('dp', 'replica')), may hold values from 0 to 224, as said below
- lengths: int32 [8], P(('dp', 'replica')), may hold values from 128 to 256, as said below
Outputs:
- prompt_final: float32 [32, 4096], P(None, 'tensor')
- weight_step: bfloat16 [4096, 2, 14336], P(('dp', 'replica'), None, 'tensor')
The draws below stay inside these ranges and needn't reach their ends.
Inputs may be any that keep to these rules, and one draw needn't show every extreme that they name: Each prompt lies inside its sequence: insert_at[b] + 32 <= lengths[b]; in every draw some prompt begins at row 0 and some prompt ends at the last row 255. `lengths`: in every draw some sequence has all 256 rows live and some has 128.
All inputs are finite; a program needn't handle non-finite values.
Results may differ from the reference program's by a relative error of at most 0.012.
Values may be sent and summed in bfloat16 or wider, within the bound.
A program may use at most 320 MiB of HBM per device.

```python
import math
import jax
import jax.numpy as jnp
from jax import lax

D = 4096
FF = 14336
NP = 32
ITERS = 3
SEQ = 256
BATCH = 8


def sequence_plan(key):
    inner_key = jax.random.fold_in(key, 11)
    key_lengths, key_longest, key_starts = jax.random.split(inner_key, 3)
    drawn_lengths = jax.random.randint(key_lengths, (BATCH,), SEQ // 2, SEQ + 1)
    longest = jax.random.randint(key_longest, (), 0, BATCH)
    shortest = (longest + 1) % BATCH
    seq_index = jnp.arange(BATCH)
    seq_lengths = jnp.where(seq_index == longest, SEQ, drawn_lengths)
    seq_lengths = jnp.where(seq_index == shortest, SEQ // 2, seq_lengths).astype(jnp.int32)
    starts = jax.random.randint(key_starts, (BATCH,), 0, seq_lengths - NP + 1)
    starts = jnp.where(seq_index == longest, SEQ - NP, starts)
    starts = jnp.where(seq_index == shortest, 0, starts)
    return (seq_lengths, starts.astype(jnp.int32))


def draw_lengths(key, part):
    return sequence_plan(key)[0]


def draw_insert_at(key, part):
    return sequence_plan(key)[1]


def draw_norm_gain(key, part):
    feature_ramp = jnp.arange(D, dtype=jnp.float32) / D
    jitter = jax.random.uniform(key, (D,), jnp.float32, -1.0, 1.0)
    return (0.35 * 10.0 ** feature_ramp * (1.0 + 0.25 * jitter)).astype(jnp.float32)


def draw_cotangent(key, part):
    key_values, key_rows = jax.random.split(key, 2)
    column_ramp = jnp.arange(FF, dtype=jnp.float32) / FF
    row_scales = 10.0 ** jax.random.uniform(key_rows, (BATCH, SEQ, 1), jnp.float32)
    values = jax.random.truncated_normal(key_values, -4.0, 4.0, (BATCH, SEQ, FF), jnp.float32)
    return (values * (0.3 * 10.0 ** column_ramp) * row_scales).astype(jnp.bfloat16)


def level_of(key, extent, cuts, low, largest):
    level, own = 1.0, jax.random.fold_in(key, 6)
    for dim, shards_of in cuts:
        steps = jnp.exp(jax.random.uniform(jax.random.fold_in(own, dim), (shards_of,), jnp.float32, low / len(cuts), largest / len(cuts)))
        level = level * jnp.repeat(steps, extent[dim] // shards_of).reshape([-1 if axis == dim else 1 for axis in range(len(extent))])
    return level


def centred(rng, extent, spread, limit, cuts=(), kind=jnp.bfloat16):
    values = jax.random.normal(rng, extent, jnp.float32) * spread
    if len(cuts) > 0:
        values = level_of(rng, extent, cuts, -0.22, 0.18) * values
    return jnp.clip(values, min=-limit, max=limit).astype(kind)


def setup_inputs(seed: int = 0) -> dict:
    keys = jax.random.split(jax.random.key(seed), 9)
    states = centred(keys[0], (BATCH, SEQ, D), 1.0, 6.0, ((0, 8),))
    norm_gain = draw_norm_gain(jax.random.fold_in(keys[8], 71), 0)
    gate_up = centred(keys[2], (D, 2, FF), D ** -0.5, 0.09375, ((0, 2), (2, 4)))
    cotangent = draw_cotangent(jax.random.fold_in(keys[8], 71), 0)
    prompt = centred(keys[4], (NP, D), 1.0, 6.0)
    step_sizes = jnp.clip(jnp.exp(jax.random.uniform(keys[5], (ITERS,), jnp.float32, math.log(0.3), math.log(1.0))), 0.3, 1.0)
    insert_at = draw_insert_at(jax.random.fold_in(keys[8], 71), 0)
    lengths = draw_lengths(jax.random.fold_in(keys[8], 71), 0)
    return dict(states=states, norm_gain=norm_gain, gate_up=gate_up, cotangent=cotangent, prompt=prompt, step_sizes=step_sizes, insert_at=insert_at, lengths=lengths)


def row_scale(feature_rows):
    return lax.rsqrt(lax.optimization_barrier(jnp.mean(feature_rows * feature_rows, axis=-1, keepdims=True)) + 1e-05)

def silu_parts(gate_values):
    sigmoid_value = jax.nn.sigmoid(gate_values)
    return (gate_values * sigmoid_value, sigmoid_value * (1.0 + gate_values * (1.0 - sigmoid_value)))

def hidden_grads(normalized, weight_pair, cotan_rows):
    unit_count = weight_pair.shape[1] // 2
    projected = jnp.dot(normalized, weight_pair, preferred_element_type=jnp.float32)
    activated, derivative = silu_parts(projected[:, :unit_count])
    up_part = projected[:, unit_count:]
    return jnp.concatenate([cotan_rows * up_part * derivative, cotan_rows * activated], axis=1).astype(jnp.bfloat16)

def norm_back(shifted, inverse_rms, norm_gain, feature_grad):
    feature_mean = lax.optimization_barrier(jnp.mean(shifted * norm_gain * feature_grad, axis=-1, keepdims=True))
    return inverse_rms * norm_gain * feature_grad - shifted * (inverse_rms * inverse_rms * inverse_rms) * feature_mean

def take_rows(seq_array, row_start):
    return lax.dynamic_slice_in_dim(seq_array, row_start.astype(jnp.int32), NP, 0)

def reference(states, norm_gain, gate_up, cotangent, prompt, step_sizes, insert_at, lengths):
    weight_pair = gate_up.reshape(D, 2 * FF)
    prompt_base = jax.vmap(take_rows)(states, insert_at).astype(jnp.float32)
    prompt_cotan = jax.vmap(take_rows)(cotangent, insert_at).astype(jnp.float32).reshape(BATCH * NP, FF)
    adversary = prompt.astype(jnp.float32)
    for attack_step in range(ITERS):
        shifted = (prompt_base + adversary[None]).reshape(BATCH * NP, D)
        inverse_rms = row_scale(shifted)
        normalized = (shifted * inverse_rms * norm_gain).astype(jnp.bfloat16)
        unit_grads = hidden_grads(normalized, weight_pair, prompt_cotan)
        feature_grad = lax.dot_general(unit_grads, weight_pair, (((1,), (1,)), ((), ())), preferred_element_type=jnp.float32)
        row_grads = norm_back(shifted, inverse_rms, norm_gain, feature_grad)
        summed_grad = lax.optimization_barrier(jnp.sum(row_grads.reshape(BATCH, NP, D), axis=0))
        adversary = adversary + step_sizes[attack_step] * summed_grad * lax.rsqrt(lax.optimization_barrier(jnp.mean(summed_grad * summed_grad, axis=-1, keepdims=True)) + 1e-06)
    slot_match = jnp.arange(SEQ, dtype=jnp.int32)[None, :, None] - insert_at[:, None, None] == jnp.arange(NP, dtype=jnp.int32)[None, None, :]
    placed = jnp.einsum('bsn,nd->bsd', slot_match.astype(jnp.float32), adversary, precision=lax.Precision.HIGHEST)
    full_rows = (states.astype(jnp.float32) + placed).reshape(BATCH * SEQ, D)
    full_normed = (full_rows * row_scale(full_rows) * norm_gain).astype(jnp.bfloat16)
    live_rows = jnp.arange(SEQ, dtype=jnp.int32)[None, :] < lengths[:, None]
    live_cotan = jnp.where(live_rows[:, :, None], cotangent.astype(jnp.float32), 0.0).reshape(BATCH * SEQ, FF)
    token_grads = hidden_grads(full_normed, weight_pair, live_cotan)
    weight_grad = lax.dot_general(full_normed, token_grads, (((0,), (0,)), ((), ())), preferred_element_type=jnp.float32)
    squares = jnp.sum(weight_grad * weight_grad)
    weight_step = (weight_grad * lax.rsqrt(squares / (2 * D * FF) + 1e-06)).astype(jnp.bfloat16).reshape(D, 2, FF)
    return (adversary, weight_step)
```

```python
import functools

import jax
import jax.numpy as jnp
from jax import lax
from jax.experimental import pallas as pl
from jax.experimental.pallas import tpu as pltpu
from jax.sharding import PartitionSpec as P

D = 4096
FF = 14336
MESH = pl.DeviceIdType.MESH


def row_scale(feature_rows):
    return lax.rsqrt(jnp.mean(feature_rows * feature_rows, axis=-1, keepdims=True) + 1e-05)


def silu_parts(gate_values):
    sigmoid_value = jax.nn.sigmoid(gate_values)
    return (
        gate_values * sigmoid_value,
        sigmoid_value * (1.0 + gate_values * (1.0 - sigmoid_value)),
    )


def hidden_grads(normalized, weight_pair, cotan_rows):
    unit_count = weight_pair.shape[1] // 2
    projected = jnp.dot(normalized, weight_pair, preferred_element_type=jnp.float32)
    activated, derivative = silu_parts(projected[:, :unit_count])
    up_part = projected[:, unit_count:]
    return jnp.concatenate(
        [cotan_rows * up_part * derivative, cotan_rows * activated], axis=1
    ).astype(jnp.bfloat16)


def step_kernel(
    tensors, chips, cores, partial_ref, adversary_ref, step_ref, out_ref,
    plane_buf, line_buf, mine, send1, recv1, send2, recv2, send3, recv3, send4, recv4,
):
    group = chips * cores
    t = lax.axis_index("tensor")
    g = lax.axis_index("dp") * cores + lax.axis_index("replica")
    rows = partial_ref.shape[0] // group
    own = rows // tensors
    plane = [lax.rem(g + k, group) for k in range(1, group)]
    line = [lax.rem(t + k, tensors) for k in range(1, tensors)]
    plane_ids = [{"dp": p // cores, "replica": lax.rem(p, cores)} for p in plane]
    line_ids = [{"tensor": p} for p in line]

    barrier = pltpu.get_barrier_semaphore()
    for device in plane_ids + line_ids:
        pl.semaphore_signal(barrier, inc=1, device_id=device, device_id_type=MESH)
    pl.semaphore_wait(barrier, group + tensors - 2)

    def exchange(pairs, ids, sends, recvs):
        copies = []
        for k, ((source, target), device) in enumerate(zip(pairs, ids)):
            copy = pltpu.make_async_remote_copy(
                src_ref=source, dst_ref=target, send_sem=sends.at[k], recv_sem=recvs.at[k],
                device_id=device, device_id_type=MESH,
            )
            copy.start()
            copies.append(copy)
        return copies

    first = exchange(
        [(partial_ref.at[pl.ds(p * rows, rows)], plane_buf.at[k]) for k, p in enumerate(plane)],
        plane_ids, send1, recv1,
    )
    total = partial_ref[pl.ds(g * rows, rows)]
    for k, copy in enumerate(first):
        copy.wait_recv()
        total = total + plane_buf[k]
    mine[...] = total
    second = exchange(
        [(mine.at[pl.ds(p * own, own)], line_buf.at[k]) for k, p in enumerate(line)],
        line_ids, send2, recv2,
    )
    grad = mine[pl.ds(t * own, own)]
    for k, copy in enumerate(second):
        copy.wait_recv()
        grad = grad + line_buf[k]
    square = jnp.sum(jnp.sum(grad * grad, axis=2, keepdims=True), axis=1, keepdims=True)
    count = partial_ref.shape[1] * partial_ref.shape[2]
    row = g * rows + t * own
    block = pl.ds(row, own)
    out_ref[block] = adversary_ref[block] + step_ref[0] * grad * lax.rsqrt(square / count + 1e-06)
    third = exchange([(out_ref.at[block], out_ref.at[block])] * len(line), line_ids, send3, recv3)
    for copy in third:
        copy.wait_recv()
    wide = pl.ds(g * rows, rows)
    fourth = exchange([(out_ref.at[wide], out_ref.at[wide])] * len(plane), plane_ids, send4, recv4)
    for copy in fourth:
        copy.wait_recv()
    for copy in first + second + third + fourth:
        copy.wait_send()


def apply_step(partial, adversary, step_size):
    tensors, chips, cores = (lax.axis_size(a) for a in ("tensor", "dp", "replica"))
    group = chips * cores
    count, width = partial.shape
    if count % (group * tensors) == 0 and width % 1024 == 0:
        shape = (count, 8, width // 8)
        rows = count // group
        own = rows // tensors
        dma = pltpu.SemaphoreType.DMA
        vmem = pl.BlockSpec(memory_space=pltpu.VMEM)
        result = pl.pallas_call(
            functools.partial(step_kernel, tensors, chips, cores),
            out_shape=jax.ShapeDtypeStruct(shape, jnp.float32),
            in_specs=[vmem, vmem, pl.BlockSpec(memory_space=pltpu.SMEM)],
            out_specs=vmem,
            scratch_shapes=[
                pltpu.VMEM((group - 1, rows) + shape[1:], jnp.float32),
                pltpu.VMEM((tensors - 1, own) + shape[1:], jnp.float32),
                pltpu.VMEM((rows,) + shape[1:], jnp.float32),
            ]
            + [dma((group - 1,))] * 2 + [dma((tensors - 1,))] * 4 + [dma((group - 1,))] * 2,
            compiler_params=pltpu.CompilerParams(
                collective_id=0, has_side_effects=True, vmem_limit_bytes=16 << 20
            ),
            name="attack_step",
        )(partial.reshape(shape), adversary.reshape(shape), step_size)
        return result.reshape(count, width)
    grad = lax.psum(partial, ("tensor", "dp", "replica"))
    scale = lax.rsqrt(jnp.mean(grad * grad, axis=-1, keepdims=True) + 1e-06)
    return adversary + step_size[0] * grad * scale


def norm_kernel(start_ref, state_ref, parts_ref, gain_ref, out_ref):
    slots = parts_ref.shape[0] // 3
    tokens = state_ref.shape[1]
    shape = (tokens, 3 * slots)
    slot = lax.broadcasted_iota(jnp.int32, shape, 0) - start_ref[pl.program_id(0)]
    column = lax.rem(lax.broadcasted_iota(jnp.int32, shape, 1), slots)
    placed = jnp.dot(
        jnp.where(slot == column, 1.0, 0.0).astype(jnp.bfloat16), parts_ref[...],
        preferred_element_type=jnp.float32,
    )
    rows = state_ref[0].astype(jnp.float32) + placed
    scale = lax.rsqrt(jnp.mean(rows * rows, axis=-1, keepdims=True) + 1e-05)
    out_ref[0] = (rows * scale * gain_ref[...]).astype(jnp.bfloat16)


def normed_rows(starts, states, parts, gain):
    count, tokens, width = states.shape
    return pl.pallas_call(
        norm_kernel,
        out_shape=jax.ShapeDtypeStruct(states.shape, jnp.bfloat16),
        grid_spec=pltpu.PrefetchScalarGridSpec(
            num_scalar_prefetch=1,
            grid=(count,),
            in_specs=[
                pl.BlockSpec((1, tokens, width), lambda b, s: (b, 0, 0)),
                pl.BlockSpec(parts.shape, lambda b, s: (0, 0)),
                pl.BlockSpec((1, width), lambda b, s: (0, 0)),
            ],
            out_specs=pl.BlockSpec((1, tokens, width), lambda b, s: (b, 0, 0)),
        ),
        compiler_params=pltpu.CompilerParams(vmem_limit_bytes=48 << 20),
        cost_estimate=pl.CostEstimate(
            flops=count * tokens * width * 200, bytes_accessed=count * tokens * width * 4,
            transcendentals=0,
        ),
        name="normed_rows",
    )(starts, states, parts, gain.reshape(1, width)).reshape(count * tokens, width)


def per_device(states, norm_gain, gate_up, cotangent, prompt, step_sizes, insert_at, lengths):
    chips, cores = lax.axis_size("dp"), lax.axis_size("replica")
    chip, core = lax.axis_index("dp"), lax.axis_index("replica")
    half, _, shard_units = gate_up.shape
    units = shard_units // chips
    count = prompt.shape[0]
    tokens = states.shape[1]
    width = half * cores

    unit_slice = lax.dynamic_slice_in_dim(gate_up, chip * units, units, 2)
    weight_pair = lax.all_gather(
        unit_slice.reshape(half, 2 * units), "replica", axis=0, tiled=True
    )

    seq_states, seq_cotan, prompt_start = states[0], cotangent[0], insert_at[0]
    package = jnp.concatenate(
        [
            lax.dynamic_slice_in_dim(seq_states, prompt_start, count, 0),
            lax.dynamic_slice_in_dim(seq_cotan, prompt_start, count, 0),
        ],
        axis=1,
    )
    package = lax.all_gather(package, "dp", axis=0, tiled=False)
    prompt_base = package[:, :, :width].astype(jnp.float32)
    prompt_cotan = (
        lax.dynamic_slice_in_dim(package, width + chip * units, units, 2)
        .reshape(chips * count, units)
        .astype(jnp.float32)
    )

    swap = [(i, (i + 1) % cores) for i in range(cores)]
    own_states = lax.all_gather(seq_states, "dp", axis=0, tiled=False)
    other_states = lax.ppermute(own_states, "replica", swap)
    own_starts = lax.all_gather(insert_at, "dp", axis=0, tiled=True)
    other_starts = lax.ppermute(own_starts, "replica", swap)
    positions = lax.broadcasted_iota(jnp.int32, (tokens, 1), 0)
    live_cotan = jnp.where(positions < lengths[0], seq_cotan, jnp.zeros_like(seq_cotan))

    def shifted_perm(k):
        return [(i, (i + k) % chips) for i in range(chips)]

    cotan_blocks = []
    for k in range(chips):
        block = lax.dynamic_slice_in_dim(live_cotan, lax.rem(chip + k, chips) * units, units, 1)
        cotan_blocks.append(lax.ppermute(block, "dp", shifted_perm(k)) if k else block)
    stacked = jnp.stack(cotan_blocks)
    token_cotan = jnp.concatenate(
        [
            lax.dynamic_index_in_dim(stacked, lax.rem(chip - j + chips, chips), 0, keepdims=False)
            for j in range(chips)
        ],
        axis=0,
    )

    adversary = prompt.astype(jnp.float32)
    for attack_step in range(step_sizes.shape[0]):
        shifted = prompt_base + adversary[None]
        inverse_rms = row_scale(shifted)
        normalized = (shifted * inverse_rms * norm_gain).astype(jnp.bfloat16)
        unit_grads = hidden_grads(normalized.reshape(chips * count, width), weight_pair, prompt_cotan)
        feature_grad = lax.dot_general(
            unit_grads, weight_pair, (((1,), (1,)), ((), ())), preferred_element_type=jnp.float32
        ).reshape(chips, count, width)
        scaled = norm_gain * feature_grad
        feature_mean = jnp.mean(shifted * scaled, axis=-1, keepdims=True)
        partial = jnp.sum(
            inverse_rms * scaled - shifted * (inverse_rms * inverse_rms * inverse_rms) * feature_mean,
            axis=0,
        )
        adversary = apply_step(partial, adversary, step_sizes[attack_step : attack_step + 1])

    high = lax.reduce_precision(adversary, 8, 7)
    middle = lax.reduce_precision(adversary - high, 8, 7)
    low = adversary - high - middle
    parts = jnp.concatenate([high, middle, low], axis=0).astype(jnp.bfloat16)
    own_normed = normed_rows(own_starts, own_states, parts, norm_gain)
    own_grads = hidden_grads(own_normed, weight_pair, token_cotan.astype(jnp.float32))
    other_grads = lax.ppermute(own_grads, "replica", swap)
    other_normed = normed_rows(other_starts, other_states, parts, norm_gain)

    block_width = width // (chips * cores)
    dims = (((0,), (0,)), ((), ()))
    squares = 0.0
    received = [None] * chips
    for k in [2 % chips, *[i for i in range(1, chips) if i != 2 % chips], 0] if chips > 2 else range(chips):
        start = (lax.rem(chip + k, chips) * cores + core) * block_width
        block = lax.dot_general(
            lax.dynamic_slice_in_dim(own_normed, start, block_width, 1), own_grads, dims,
            preferred_element_type=jnp.float32,
        ) + lax.dot_general(
            lax.dynamic_slice_in_dim(other_normed, start, block_width, 1), other_grads, dims,
            preferred_element_type=jnp.float32,
        )
        squares = squares + jnp.sum(block * block)
        sent = block.astype(jnp.bfloat16)
        received[k] = lax.ppermute(sent, "dp", shifted_perm(k)) if k else sent
    squares = lax.psum(squares, ("tensor", "dp", "replica"))
    scale = lax.rsqrt(squares / (2 * D * FF) + 1e-06)
    stacked = jnp.stack(received)
    pieces = [
        lax.dynamic_index_in_dim(stacked, lax.rem(chip - j + chips, chips), 0, keepdims=False)
        for j in range(chips)
    ]
    weight_step = jnp.concatenate(
        [piece.reshape(block_width, 2, units) for piece in pieces], axis=2
    )
    weight_step = (weight_step.astype(jnp.float32) * scale).astype(jnp.bfloat16)
    column_count = width // lax.axis_size("tensor")
    prompt_final = lax.dynamic_slice_in_dim(
        adversary, lax.axis_index("tensor") * column_count, column_count, 1
    )
    return (prompt_final, weight_step)


def solution(mesh):
    return jax.shard_map(
        per_device,
        mesh=mesh,
        in_specs=(
            P(("dp", "replica"), None, None),
            P(),
            P("replica", None, "tensor"),
            P(("dp", "replica"), None, "tensor"),
            P(),
            P(),
            P(("dp", "replica")),
            P(("dp", "replica")),
        ),
        out_specs=(P(None, "tensor"), P(("dp", "replica"), None, "tensor")),
        check_vma=False,
    )
```

```python
import functools

import jax
import jax.numpy as jnp
from jax import lax
from jax.experimental import pallas as pl
from jax.experimental.pallas import tpu as pltpu
from jax.sharding import PartitionSpec as P

D = 4096
FF = 14336
MESH = pl.DeviceIdType.MESH


def row_scale(feature_rows):
    return lax.rsqrt(jnp.mean(feature_rows * feature_rows, axis=-1, keepdims=True) + 1e-05)


def silu_parts(gate_values):
    sigmoid_value = jax.nn.sigmoid(gate_values)
    return (
        gate_values * sigmoid_value,
        sigmoid_value * (1.0 + gate_values * (1.0 - sigmoid_value)),
    )


def hidden_grads(normalized, weight_pair, cotan_rows):
    unit_count = weight_pair.shape[1] // 2
    projected = jnp.dot(normalized, weight_pair, preferred_element_type=jnp.float32)
    activated, derivative = silu_parts(projected[:, :unit_count])
    up_part = projected[:, unit_count:]
    return jnp.concatenate(
        [cotan_rows * up_part * derivative, cotan_rows * activated], axis=1
    ).astype(jnp.bfloat16)


def step_kernel(
    tensors, chips, cores, partial_ref, adversary_ref, step_ref, out_ref,
    plane_buf, line_buf, mine, send1, recv1, send2, recv2, send3, recv3, send4, recv4,
):
    group = chips * cores
    t = lax.axis_index("tensor")
    g = lax.axis_index("dp") * cores + lax.axis_index("replica")
    rows = partial_ref.shape[0] // group
    own = rows // tensors
    plane = [lax.rem(g + k, group) for k in range(1, group)]
    line = [lax.rem(t + k, tensors) for k in range(1, tensors)]
    plane_ids = [{"dp": p // cores, "replica": lax.rem(p, cores)} for p in plane]
    line_ids = [{"tensor": p} for p in line]

    barrier = pltpu.get_barrier_semaphore()
    for device in plane_ids + line_ids:
        pl.semaphore_signal(barrier, inc=1, device_id=device, device_id_type=MESH)
    pl.semaphore_wait(barrier, group + tensors - 2)

    def exchange(pairs, ids, sends, recvs):
        copies = []
        for k, ((source, target), device) in enumerate(zip(pairs, ids)):
            copy = pltpu.make_async_remote_copy(
                src_ref=source, dst_ref=target, send_sem=sends.at[k], recv_sem=recvs.at[k],
                device_id=device, device_id_type=MESH,
            )
            copy.start()
            copies.append(copy)
        return copies

    first = exchange(
        [(partial_ref.at[pl.ds(p * rows, rows)], plane_buf.at[k]) for k, p in enumerate(plane)],
        plane_ids, send1, recv1,
    )
    total = partial_ref[pl.ds(g * rows, rows)]
    for k, copy in enumerate(first):
        copy.wait_recv()
        total = total + plane_buf[k]
    mine[...] = total
    second = exchange(
        [(mine.at[pl.ds(p * own, own)], line_buf.at[k]) for k, p in enumerate(line)],
        line_ids, send2, recv2,
    )
    grad = mine[pl.ds(t * own, own)]
    for k, copy in enumerate(second):
        copy.wait_recv()
        grad = grad + line_buf[k]
    square = jnp.sum(jnp.sum(grad * grad, axis=2, keepdims=True), axis=1, keepdims=True)
    count = partial_ref.shape[1] * partial_ref.shape[2]
    row = g * rows + t * own
    block = pl.ds(row, own)
    out_ref[block] = adversary_ref[block] + step_ref[0] * grad * lax.rsqrt(square / count + 1e-06)
    third = exchange([(out_ref.at[block], out_ref.at[block])] * len(line), line_ids, send3, recv3)
    for copy in third:
        copy.wait_recv()
    wide = pl.ds(g * rows, rows)
    fourth = exchange([(out_ref.at[wide], out_ref.at[wide])] * len(plane), plane_ids, send4, recv4)
    for copy in fourth:
        copy.wait_recv()
    for copy in first + second + third + fourth:
        copy.wait_send()


def apply_step(partial, adversary, step_size):
    tensors, chips, cores = (lax.axis_size(a) for a in ("tensor", "dp", "replica"))
    group = chips * cores
    count, width = partial.shape
    if count % (group * tensors) == 0 and width % 1024 == 0:
        shape = (count, 8, width // 8)
        rows = count // group
        own = rows // tensors
        dma = pltpu.SemaphoreType.DMA
        vmem = pl.BlockSpec(memory_space=pltpu.VMEM)
        result = pl.pallas_call(
            functools.partial(step_kernel, tensors, chips, cores),
            out_shape=jax.ShapeDtypeStruct(shape, jnp.float32),
            in_specs=[vmem, vmem, pl.BlockSpec(memory_space=pltpu.SMEM)],
            out_specs=vmem,
            scratch_shapes=[
                pltpu.VMEM((group - 1, rows) + shape[1:], jnp.float32),
                pltpu.VMEM((tensors - 1, own) + shape[1:], jnp.float32),
                pltpu.VMEM((rows,) + shape[1:], jnp.float32),
            ]
            + [dma((group - 1,))] * 2 + [dma((tensors - 1,))] * 4 + [dma((group - 1,))] * 2,
            compiler_params=pltpu.CompilerParams(
                collective_id=0, has_side_effects=True, vmem_limit_bytes=16 << 20
            ),
            cost_estimate=pl.CostEstimate(
                flops=20_000_000_000, bytes_accessed=3 * count * width * 4, transcendentals=0
            ),
            name="attack_step",
        )(partial.reshape(shape), adversary.reshape(shape), step_size)
        return result.reshape(count, width)
    grad = lax.psum(partial, ("tensor", "dp", "replica"))
    scale = lax.rsqrt(jnp.mean(grad * grad, axis=-1, keepdims=True) + 1e-06)
    return adversary + step_size[0] * grad * scale


def scalar_kernel(tensors, chips, cores, value_ref, out_ref, buf1, buf2, mine, send1, recv1, send2, recv2):
    group = chips * cores
    t = lax.axis_index("tensor")
    g = lax.axis_index("dp") * cores + lax.axis_index("replica")
    plane = [lax.rem(g + k, group) for k in range(1, group)]
    plane_ids = [{"dp": p // cores, "replica": lax.rem(p, cores)} for p in plane]
    line_ids = [{"tensor": lax.rem(t + k, tensors)} for k in range(1, tensors)]
    barrier = pltpu.get_barrier_semaphore()
    for device in plane_ids + line_ids:
        pl.semaphore_signal(barrier, inc=1, device_id=device, device_id_type=MESH)
    pl.semaphore_wait(barrier, group + tensors - 2)
    copies = []
    total = value_ref[...]
    source = value_ref
    for ids, buf, sends, recvs in ((plane_ids, buf1, send1, recv1), (line_ids, buf2, send2, recv2)):
        stage = []
        for k, device in enumerate(ids):
            copy = pltpu.make_async_remote_copy(
                src_ref=source, dst_ref=buf.at[k], send_sem=sends.at[k], recv_sem=recvs.at[k],
                device_id=device, device_id_type=MESH,
            )
            copy.start()
            stage.append(copy)
        for k, copy in enumerate(stage):
            copy.wait_recv()
            total = total + buf[k]
        copies += stage
        if buf is buf1:
            mine[...] = total
            source = mine
    out_ref[...] = total
    for copy in copies:
        copy.wait_send()


def sum_everywhere(value):
    tensors, chips, cores = (lax.axis_size(a) for a in ("tensor", "dp", "replica"))
    group = chips * cores
    if not 1 < tensors <= 8 or not 1 < group <= 16:
        return lax.psum(value, ("tensor", "dp", "replica"))
    dma = pltpu.SemaphoreType.DMA
    vmem = pl.BlockSpec(memory_space=pltpu.VMEM)
    return pl.pallas_call(
        functools.partial(scalar_kernel, tensors, chips, cores),
        out_shape=jax.ShapeDtypeStruct((8, 128), jnp.float32),
        in_specs=[vmem],
        out_specs=vmem,
        scratch_shapes=[
            pltpu.VMEM((group - 1, 8, 128), jnp.float32),
            pltpu.VMEM((tensors - 1, 8, 128), jnp.float32),
            pltpu.VMEM((8, 128), jnp.float32),
        ]
        + [dma((group - 1,))] * 2 + [dma((tensors - 1,))] * 2,
        compiler_params=pltpu.CompilerParams(
            collective_id=1, has_side_effects=True, vmem_limit_bytes=4 << 20
        ),
        name="scalar_sum",
    )(jnp.full((8, 128), value, jnp.float32))[0, 0]


def norm_kernel(start_ref, state_ref, parts_ref, gain_ref, out_ref):
    slots = parts_ref.shape[0] // 3
    tokens = state_ref.shape[1]
    shape = (tokens, 3 * slots)
    slot = lax.broadcasted_iota(jnp.int32, shape, 0) - start_ref[pl.program_id(0)]
    column = lax.rem(lax.broadcasted_iota(jnp.int32, shape, 1), slots)
    placed = jnp.dot(
        jnp.where(slot == column, 1.0, 0.0).astype(jnp.bfloat16), parts_ref[...],
        preferred_element_type=jnp.float32,
    )
    rows = state_ref[0].astype(jnp.float32) + placed
    scale = lax.rsqrt(jnp.mean(rows * rows, axis=-1, keepdims=True) + 1e-05)
    out_ref[0] = (rows * scale * gain_ref[...]).astype(jnp.bfloat16)


def normed_rows(starts, states, parts, gain):
    count, tokens, width = states.shape
    return pl.pallas_call(
        norm_kernel,
        out_shape=jax.ShapeDtypeStruct(states.shape, jnp.bfloat16),
        grid_spec=pltpu.PrefetchScalarGridSpec(
            num_scalar_prefetch=1,
            grid=(count,),
            in_specs=[
                pl.BlockSpec((1, tokens, width), lambda b, s: (b, 0, 0)),
                pl.BlockSpec(parts.shape, lambda b, s: (0, 0)),
                pl.BlockSpec((1, width), lambda b, s: (0, 0)),
            ],
            out_specs=pl.BlockSpec((1, tokens, width), lambda b, s: (b, 0, 0)),
        ),
        compiler_params=pltpu.CompilerParams(vmem_limit_bytes=48 << 20),
        cost_estimate=pl.CostEstimate(
            flops=count * tokens * width * 200, bytes_accessed=count * tokens * width * 4,
            transcendentals=0,
        ),
        name="normed_rows",
    )(starts, states, parts, gain.reshape(1, width)).reshape(count * tokens, width)


def per_device(states, norm_gain, gate_up, cotangent, prompt, step_sizes, insert_at, lengths):
    chips, cores = lax.axis_size("dp"), lax.axis_size("replica")
    chip, core = lax.axis_index("dp"), lax.axis_index("replica")
    half, _, shard_units = gate_up.shape
    units = shard_units // chips
    count = prompt.shape[0]
    tokens = states.shape[1]
    width = half * cores

    unit_slice = lax.dynamic_slice_in_dim(gate_up, chip * units, units, 2)
    weight_pair = lax.all_gather(
        unit_slice.reshape(half, 2 * units), "replica", axis=0, tiled=True
    )

    seq_states, seq_cotan, prompt_start = states[0], cotangent[0], insert_at[0]
    package = jnp.concatenate(
        [
            lax.dynamic_slice_in_dim(seq_states, prompt_start, count, 0),
            lax.dynamic_slice_in_dim(seq_cotan, prompt_start, count, 0),
            jnp.broadcast_to(insert_at.astype(jnp.bfloat16).reshape(1, 1), (count, 128)),
        ],
        axis=1,
    )
    package = lax.all_gather(package, "dp", axis=0, tiled=False)
    prompt_base = package[:, :, :width].astype(jnp.float32)
    prompt_cotan = (
        lax.dynamic_slice_in_dim(package, width + chip * units, units, 2)
        .reshape(chips * count, units)
        .astype(jnp.float32)
    )

    swap = [(i, (i + 1) % cores) for i in range(cores)]
    own_starts = package[:, 0, package.shape[2] - 1].astype(jnp.int32)
    seq_states, seq_cotan, _ = lax.optimization_barrier((seq_states, seq_cotan, weight_pair))
    own_states = lax.all_gather(seq_states, "dp", axis=0, tiled=False)
    other_starts = lax.ppermute(own_starts, "replica", swap)
    positions = lax.broadcasted_iota(jnp.int32, (tokens, 1), 0)
    live_cotan = jnp.where(positions < lengths[0], seq_cotan, jnp.zeros_like(seq_cotan))

    def shifted_perm(k):
        return [(i, (i + k) % chips) for i in range(chips)]

    cotan_blocks = []
    for k in range(chips):
        block = lax.dynamic_slice_in_dim(live_cotan, lax.rem(chip + k, chips) * units, units, 1)
        cotan_blocks.append(lax.ppermute(block, "dp", shifted_perm(k)) if k else block)
    stacked = jnp.stack(cotan_blocks)
    token_cotan = jnp.concatenate(
        [
            lax.dynamic_index_in_dim(stacked, lax.rem(chip - j + chips, chips), 0, keepdims=False)
            for j in range(chips)
        ],
        axis=0,
    )

    adversary = prompt.astype(jnp.float32)
    for attack_step in range(step_sizes.shape[0]):
        shifted = prompt_base + adversary[None]
        inverse_rms = row_scale(shifted)
        normalized = (shifted * inverse_rms * norm_gain).astype(jnp.bfloat16)
        unit_grads = hidden_grads(normalized.reshape(chips * count, width), weight_pair, prompt_cotan)
        feature_grad = lax.dot_general(
            unit_grads, weight_pair, (((1,), (1,)), ((), ())), preferred_element_type=jnp.float32
        ).reshape(chips, count, width)
        scaled = norm_gain * feature_grad
        feature_mean = jnp.mean(shifted * scaled, axis=-1, keepdims=True)
        partial = jnp.sum(
            inverse_rms * scaled - shifted * (inverse_rms * inverse_rms * inverse_rms) * feature_mean,
            axis=0,
        )
        adversary = apply_step(partial, adversary, step_sizes[attack_step : attack_step + 1])
        if attack_step == step_sizes.shape[0] - 2:
            own_states, adversary = lax.optimization_barrier((own_states, adversary))
            other_states = lax.ppermute(own_states, "replica", swap)

    high = lax.reduce_precision(adversary, 8, 7)
    middle = lax.reduce_precision(adversary - high, 8, 7)
    low = adversary - high - middle
    parts = jnp.concatenate([high, middle, low], axis=0).astype(jnp.bfloat16)
    own_normed = normed_rows(own_starts, own_states, parts, norm_gain)
    own_grads = hidden_grads(own_normed, weight_pair, token_cotan.astype(jnp.float32))
    other_grads = lax.ppermute(own_grads, "replica", swap)
    other_normed = normed_rows(other_starts, other_states, parts, norm_gain)

    block_width = width // (chips * cores)
    dims = (((0,), (0,)), ((), ()))
    squares = 0.0
    received = [None] * chips
    for k in [2 % chips, *[i for i in range(1, chips) if i != 2 % chips], 0] if chips > 2 else range(chips):
        start = (lax.rem(chip + k, chips) * cores + core) * block_width
        block = lax.dot_general(
            lax.dynamic_slice_in_dim(own_normed, start, block_width, 1), own_grads, dims,
            preferred_element_type=jnp.float32,
        ) + lax.dot_general(
            lax.dynamic_slice_in_dim(other_normed, start, block_width, 1), other_grads, dims,
            preferred_element_type=jnp.float32,
        )
        squares = squares + jnp.sum(block * block)
        sent = block.astype(jnp.bfloat16).reshape(block_width, 2, units)
        received[k] = lax.ppermute(sent, "dp", shifted_perm(k)) if k else sent
    squares = sum_everywhere(squares)
    scale = lax.rsqrt(squares / (2 * D * FF) + 1e-06)
    stacked = jnp.stack(received)
    pieces = [
        lax.dynamic_index_in_dim(stacked, lax.rem(chip - j + chips, chips), 0, keepdims=False)
        for j in range(chips)
    ]
    weight_step = jnp.concatenate(
        pieces, axis=2
    )
    weight_step = (weight_step.astype(jnp.float32) * scale).astype(jnp.bfloat16)
    column_count = width // lax.axis_size("tensor")
    prompt_final = lax.dynamic_slice_in_dim(
        adversary, lax.axis_index("tensor") * column_count, column_count, 1
    )
    return (prompt_final, weight_step)


def solution(mesh):
    return jax.shard_map(
        per_device,
        mesh=mesh,
        in_specs=(
            P(("dp", "replica"), None, None),
            P(),
            P("replica", None, "tensor"),
            P(("dp", "replica"), None, "tensor"),
            P(),
            P(),
            P(("dp", "replica")),
            P(("dp", "replica")),
        ),
        out_specs=(P(None, "tensor"), P(("dp", "replica"), None, "tensor")),
        check_vma=False,
    )
```

```python
import functools

import jax
import jax.numpy as jnp
from jax import lax
from jax.experimental import pallas as pl
from jax.experimental.pallas import tpu as pltpu
from jax.sharding import PartitionSpec as P

D = 4096
FF = 14336
MESH = pl.DeviceIdType.MESH


def row_scale(feature_rows):
    return lax.rsqrt(jnp.mean(feature_rows * feature_rows, axis=-1, keepdims=True) + 1e-05)


def silu_parts(gate_values):
    sigmoid_value = jax.nn.sigmoid(gate_values)
    return (
        gate_values * sigmoid_value,
        sigmoid_value * (1.0 + gate_values * (1.0 - sigmoid_value)),
    )


def hidden_grads(normalized, weight_pair, cotan_rows):
    unit_count = weight_pair.shape[1] // 2
    projected = jnp.dot(normalized, weight_pair, preferred_element_type=jnp.float32)
    activated, derivative = silu_parts(projected[:, :unit_count])
    up_part = projected[:, unit_count:]
    return jnp.concatenate(
        [cotan_rows * up_part * derivative, cotan_rows * activated], axis=1
    ).astype(jnp.bfloat16)


def step_kernel(
    tensors, chips, cores, partial_ref, adversary_ref, step_ref, out_ref,
    plane_buf, line_buf, mine, send1, recv1, send2, recv2, send3, recv3, send4, recv4,
):
    group = chips * cores
    t = lax.axis_index("tensor")
    g = lax.axis_index("dp") * cores + lax.axis_index("replica")
    rows = partial_ref.shape[0] // group
    own = rows // tensors
    plane = [lax.rem(g + k, group) for k in range(1, group)]
    line = [lax.rem(t + k, tensors) for k in range(1, tensors)]
    plane_ids = [{"dp": p // cores, "replica": lax.rem(p, cores)} for p in plane]
    line_ids = [{"tensor": p} for p in line]

    barrier = pltpu.get_barrier_semaphore()
    for device in plane_ids + line_ids:
        pl.semaphore_signal(barrier, inc=1, device_id=device, device_id_type=MESH)
    pl.semaphore_wait(barrier, group + tensors - 2)

    def exchange(pairs, ids, sends, recvs):
        copies = []
        for k, ((source, target), device) in enumerate(zip(pairs, ids)):
            copy = pltpu.make_async_remote_copy(
                src_ref=source, dst_ref=target, send_sem=sends.at[k], recv_sem=recvs.at[k],
                device_id=device, device_id_type=MESH,
            )
            copy.start()
            copies.append(copy)
        return copies

    first = exchange(
        [(partial_ref.at[pl.ds(p * rows, rows)], plane_buf.at[k]) for k, p in enumerate(plane)],
        plane_ids, send1, recv1,
    )
    total = partial_ref[pl.ds(g * rows, rows)]
    for k, copy in enumerate(first):
        copy.wait_recv()
        total = total + plane_buf[k]
    mine[...] = total
    second = exchange(
        [(mine.at[pl.ds(p * own, own)], line_buf.at[k]) for k, p in enumerate(line)],
        line_ids, send2, recv2,
    )
    grad = mine[pl.ds(t * own, own)]
    for k, copy in enumerate(second):
        copy.wait_recv()
        grad = grad + line_buf[k]
    square = jnp.sum(jnp.sum(grad * grad, axis=2, keepdims=True), axis=1, keepdims=True)
    count = partial_ref.shape[1] * partial_ref.shape[2]
    row = g * rows + t * own
    block = pl.ds(row, own)
    out_ref[block] = adversary_ref[block] + step_ref[0] * grad * lax.rsqrt(square / count + 1e-06)
    third = exchange([(out_ref.at[block], out_ref.at[block])] * len(line), line_ids, send3, recv3)
    for copy in third:
        copy.wait_recv()
    wide = pl.ds(g * rows, rows)
    fourth = exchange([(out_ref.at[wide], out_ref.at[wide])] * len(plane), plane_ids, send4, recv4)
    for copy in fourth:
        copy.wait_recv()
    for copy in first + second + third + fourth:
        copy.wait_send()


def apply_step(partial, adversary, step_size):
    tensors, chips, cores = (lax.axis_size(a) for a in ("tensor", "dp", "replica"))
    group = chips * cores
    count, width = partial.shape
    if count % (group * tensors) == 0 and width % 1024 == 0:
        shape = (count, 8, width // 8)
        rows = count // group
        own = rows // tensors
        dma = pltpu.SemaphoreType.DMA
        vmem = pl.BlockSpec(memory_space=pltpu.VMEM)
        result = pl.pallas_call(
            functools.partial(step_kernel, tensors, chips, cores),
            out_shape=jax.ShapeDtypeStruct(shape, jnp.float32),
            in_specs=[vmem, vmem, pl.BlockSpec(memory_space=pltpu.SMEM)],
            out_specs=vmem,
            scratch_shapes=[
                pltpu.VMEM((group - 1, rows) + shape[1:], jnp.float32),
                pltpu.VMEM((tensors - 1, own) + shape[1:], jnp.float32),
                pltpu.VMEM((rows,) + shape[1:], jnp.float32),
            ]
            + [dma((group - 1,))] * 2 + [dma((tensors - 1,))] * 4 + [dma((group - 1,))] * 2,
            compiler_params=pltpu.CompilerParams(
                collective_id=0, has_side_effects=True, vmem_limit_bytes=16 << 20
            ),
            cost_estimate=pl.CostEstimate(
                flops=20_000_000_000, bytes_accessed=3 * count * width * 4, transcendentals=0
            ),
            name="attack_step",
        )(partial.reshape(shape), adversary.reshape(shape), step_size)
        return result.reshape(count, width)
    grad = lax.psum(partial, ("tensor", "dp", "replica"))
    scale = lax.rsqrt(jnp.mean(grad * grad, axis=-1, keepdims=True) + 1e-06)
    return adversary + step_size[0] * grad * scale


def scalar_kernel(tensors, chips, cores, value_ref, out_ref, buf1, buf2, mine, send1, recv1, send2, recv2):
    group = chips * cores
    t = lax.axis_index("tensor")
    g = lax.axis_index("dp") * cores + lax.axis_index("replica")
    plane = [lax.rem(g + k, group) for k in range(1, group)]
    plane_ids = [{"dp": p // cores, "replica": lax.rem(p, cores)} for p in plane]
    line_ids = [{"tensor": lax.rem(t + k, tensors)} for k in range(1, tensors)]
    barrier = pltpu.get_barrier_semaphore()
    for device in plane_ids + line_ids:
        pl.semaphore_signal(barrier, inc=1, device_id=device, device_id_type=MESH)
    pl.semaphore_wait(barrier, group + tensors - 2)
    copies = []
    total = value_ref[...]
    source = value_ref
    for ids, buf, sends, recvs in ((plane_ids, buf1, send1, recv1), (line_ids, buf2, send2, recv2)):
        stage = []
        for k, device in enumerate(ids):
            copy = pltpu.make_async_remote_copy(
                src_ref=source, dst_ref=buf.at[k], send_sem=sends.at[k], recv_sem=recvs.at[k],
                device_id=device, device_id_type=MESH,
            )
            copy.start()
            stage.append(copy)
        for k, copy in enumerate(stage):
            copy.wait_recv()
            total = total + buf[k]
        copies += stage
        if buf is buf1:
            mine[...] = total
            source = mine
    out_ref[...] = total
    for copy in copies:
        copy.wait_send()


def sum_everywhere(value):
    tensors, chips, cores = (lax.axis_size(a) for a in ("tensor", "dp", "replica"))
    group = chips * cores
    if not 1 < tensors <= 8 or not 1 < group <= 16:
        return lax.psum(value, ("tensor", "dp", "replica"))
    dma = pltpu.SemaphoreType.DMA
    vmem = pl.BlockSpec(memory_space=pltpu.VMEM)
    return pl.pallas_call(
        functools.partial(scalar_kernel, tensors, chips, cores),
        out_shape=jax.ShapeDtypeStruct((8, 128), jnp.float32),
        in_specs=[vmem],
        out_specs=vmem,
        scratch_shapes=[
            pltpu.VMEM((group - 1, 8, 128), jnp.float32),
            pltpu.VMEM((tensors - 1, 8, 128), jnp.float32),
            pltpu.VMEM((8, 128), jnp.float32),
        ]
        + [dma((group - 1,))] * 2 + [dma((tensors - 1,))] * 2,
        compiler_params=pltpu.CompilerParams(
            collective_id=1, has_side_effects=True, vmem_limit_bytes=4 << 20
        ),
        name="scalar_sum",
    )(jnp.full((8, 128), value, jnp.float32))[0, 0]


def norm_kernel(start_ref, state_ref, parts_ref, gain_ref, out_ref):
    slots = parts_ref.shape[0] // 3
    tokens = state_ref.shape[1]
    shape = (tokens, 3 * slots)
    slot = lax.broadcasted_iota(jnp.int32, shape, 0) - start_ref[pl.program_id(0)]
    column = lax.rem(lax.broadcasted_iota(jnp.int32, shape, 1), slots)
    placed = jnp.dot(
        jnp.where(slot == column, 1.0, 0.0).astype(jnp.bfloat16), parts_ref[...],
        preferred_element_type=jnp.float32,
    )
    rows = state_ref[0].astype(jnp.float32) + placed
    scale = lax.rsqrt(jnp.mean(rows * rows, axis=-1, keepdims=True) + 1e-05)
    out_ref[0] = (rows * scale * gain_ref[...]).astype(jnp.bfloat16)


def normed_rows(starts, states, parts, gain):
    count, tokens, width = states.shape
    return pl.pallas_call(
        norm_kernel,
        out_shape=jax.ShapeDtypeStruct(states.shape, jnp.bfloat16),
        grid_spec=pltpu.PrefetchScalarGridSpec(
            num_scalar_prefetch=1,
            grid=(count,),
            in_specs=[
                pl.BlockSpec((1, tokens, width), lambda b, s: (b, 0, 0)),
                pl.BlockSpec(parts.shape, lambda b, s: (0, 0)),
                pl.BlockSpec((1, width), lambda b, s: (0, 0)),
            ],
            out_specs=pl.BlockSpec((1, tokens, width), lambda b, s: (b, 0, 0)),
        ),
        compiler_params=pltpu.CompilerParams(vmem_limit_bytes=48 << 20),
        cost_estimate=pl.CostEstimate(
            flops=count * tokens * width * 200, bytes_accessed=count * tokens * width * 4,
            transcendentals=0,
        ),
        name="normed_rows",
    )(starts, states, parts, gain.reshape(1, width)).reshape(count * tokens, width)


def per_device(states, norm_gain, gate_up, cotangent, prompt, step_sizes, insert_at, lengths):
    chips, cores = lax.axis_size("dp"), lax.axis_size("replica")
    chip, core = lax.axis_index("dp"), lax.axis_index("replica")
    half, _, shard_units = gate_up.shape
    units = shard_units // chips
    count = prompt.shape[0]
    tokens = states.shape[1]
    width = half * cores

    unit_slice = lax.dynamic_slice_in_dim(gate_up, chip * units, units, 2)
    weight_pair = lax.all_gather(
        unit_slice.reshape(half, 2 * units), "replica", axis=0, tiled=True
    )

    seq_states, seq_cotan, prompt_start = states[0], cotangent[0], insert_at[0]
    package = jnp.concatenate(
        [
            lax.dynamic_slice_in_dim(seq_states, prompt_start, count, 0),
            lax.dynamic_slice_in_dim(seq_cotan, prompt_start, count, 0),
            jnp.broadcast_to(insert_at.astype(jnp.bfloat16).reshape(1, 1), (count, 128)),
        ],
        axis=1,
    )
    package = lax.all_gather(package, "dp", axis=0, tiled=False)
    prompt_base = package[:, :, :width].astype(jnp.float32)
    prompt_cotan = (
        lax.dynamic_slice_in_dim(package, width + chip * units, units, 2)
        .reshape(chips * count, units)
        .astype(jnp.float32)
    )

    swap = [(i, (i + 1) % cores) for i in range(cores)]
    own_starts = package[:, 0, package.shape[2] - 1].astype(jnp.int32)
    seq_states, seq_cotan, _ = lax.optimization_barrier((seq_states, seq_cotan, weight_pair))
    own_states = lax.all_gather(seq_states, "dp", axis=0, tiled=False)
    other_starts = lax.ppermute(own_starts, "replica", swap)
    positions = lax.broadcasted_iota(jnp.int32, (tokens, 1), 0)
    live_cotan = jnp.where(positions < lengths[0], seq_cotan, jnp.zeros_like(seq_cotan))

    def shifted_perm(k):
        return [(i, (i + k) % chips) for i in range(chips)]

    cotan_blocks = []
    for k in range(chips):
        block = lax.dynamic_slice_in_dim(live_cotan, lax.rem(chip + k, chips) * units, units, 1)
        cotan_blocks.append(lax.ppermute(block, "dp", shifted_perm(k)) if k else block)
    stacked = jnp.stack(cotan_blocks)
    token_cotan = jnp.concatenate(
        [
            lax.dynamic_index_in_dim(stacked, lax.rem(chip - j + chips, chips), 0, keepdims=False)
            for j in range(chips)
        ],
        axis=0,
    )

    adversary = prompt.astype(jnp.float32)
    for attack_step in range(step_sizes.shape[0]):
        shifted = prompt_base + adversary[None]
        inverse_rms = row_scale(shifted)
        normalized = (shifted * inverse_rms * norm_gain).astype(jnp.bfloat16)
        unit_grads = hidden_grads(normalized.reshape(chips * count, width), weight_pair, prompt_cotan)
        feature_grad = lax.dot_general(
            unit_grads, weight_pair, (((1,), (1,)), ((), ())), preferred_element_type=jnp.float32
        ).reshape(chips, count, width)
        scaled = norm_gain * feature_grad
        feature_mean = jnp.mean(shifted * scaled, axis=-1, keepdims=True)
        partial = jnp.sum(
            inverse_rms * scaled - shifted * (inverse_rms * inverse_rms * inverse_rms) * feature_mean,
            axis=0,
        )
        adversary = apply_step(partial, adversary, step_sizes[attack_step : attack_step + 1])
        if attack_step == step_sizes.shape[0] - 2:
            own_states, adversary = lax.optimization_barrier((own_states, adversary))
            other_states = lax.ppermute(own_states, "replica", swap)

    high = lax.reduce_precision(adversary, 8, 7)
    middle = lax.reduce_precision(adversary - high, 8, 7)
    low = adversary - high - middle
    parts = jnp.concatenate([high, middle, low], axis=0).astype(jnp.bfloat16)
    own_normed = normed_rows(own_starts, own_states, parts, norm_gain)
    own_grads = hidden_grads(own_normed, weight_pair, token_cotan.astype(jnp.float32))
    other_grads = lax.ppermute(own_grads, "replica", swap)
    other_normed = normed_rows(other_starts, other_states, parts, norm_gain)

    block_width = width // (chips * cores)
    dims = (((0,), (0,)), ((), ()))
    squares = 0.0
    received = [None] * chips
    for k in [2 % chips, *[i for i in range(1, chips) if i != 2 % chips], 0] if chips > 2 else range(chips):
        start = (lax.rem(chip + k, chips) * cores + core) * block_width
        block = lax.dot_general(
            lax.dynamic_slice_in_dim(own_normed, start, block_width, 1), own_grads, dims,
            preferred_element_type=jnp.float32,
        ) + lax.dot_general(
            lax.dynamic_slice_in_dim(other_normed, start, block_width, 1), other_grads, dims,
            preferred_element_type=jnp.float32,
        )
        squares = squares + jnp.sum(block * block)
        sent = block.astype(jnp.bfloat16)
        received[k] = lax.ppermute(sent, "dp", shifted_perm(k)) if k else sent
    squares = sum_everywhere(squares)
    scale = lax.rsqrt(squares / (2 * D * FF) + 1e-06)
    stacked = jnp.stack(received)
    pieces = [
        lax.dynamic_index_in_dim(stacked, lax.rem(chip - j + chips, chips), 0, keepdims=False)
        for j in range(chips)
    ]
    weight_step = jnp.concatenate(
        [piece.reshape(block_width, 2, units) for piece in pieces], axis=2
    )
    weight_step = (weight_step.astype(jnp.float32) * scale).astype(jnp.bfloat16)
    column_count = width // lax.axis_size("tensor")
    prompt_final = lax.dynamic_slice_in_dim(
        adversary, lax.axis_index("tensor") * column_count, column_count, 1
    )
    return (prompt_final, weight_step)


def solution(mesh):
    return jax.shard_map(
        per_device,
        mesh=mesh,
        in_specs=(
            P(("dp", "replica"), None, None),
            P(),
            P("replica", None, "tensor"),
            P(("dp", "replica"), None, "tensor"),
            P(),
            P(),
            P(("dp", "replica")),
            P(("dp", "replica")),
        ),
        out_specs=(P(None, "tensor"), P(("dp", "replica"), None, "tensor")),
        check_vma=False,
    )
```
